32 devices in a mesh: row: 16 (over z, y, core), col: 2 (over x).
Axes of the slice: x: 2, y: 2, z: 4, core: 2. Of those that a mesh axis runs over, the one named last changes fastest.
Arguments:
- hidden: bfloat16 [2048, 1152], P('col', 'row'), may hold values from -6 to 6
- caption: bfloat16 [1920, 1152], P('col', 'row'), may hold values from -6 to 6
- lengths: int32 [16], replicated, may hold values from 1 to 120, as said below
- timesteps: int32 [16], replicated, may hold values from 0 to 999
- time_table: float32 [6, 1152, 1000], P(None, 'row'), may hold values from -2 to 2
- shift_table: float32 [6, 1152], P(None, 'row'), may hold values from -2 to 2
- query_weight: bfloat16 [1152, 1152], P('row', 'col'), may hold values from -0.1875 to 0.1875
- query_offset: float32 [1152], P('col'), may hold values from -3 to 3
- key_weight: bfloat16 [1152, 1152], P('row', 'col'), may hold values from -0.1875 to 0.1875
- value_weight: bfloat16 [1152, 1152], P('row', 'col'), may hold values from -0.1875 to 0.1875
- value_offset: float32 [1152], P('col'), may hold values from -3 to 3
- output_weight: bfloat16 [1152, 1152], P('col', 'row'), may hold values from -1 to 1
- output_offset: float32 [1152], P('row'), may hold values from -3 to 3
- probe_weight: bfloat16 [1152, 1152], P('row', 'col'), may hold values from -0.1875 to 0.1875
- probe_offset: float32 [1152], P('col'), may hold values from -3 to 3
- lookup_weight: bfloat16 [1152, 1152], P('row', 'col'), may hold values from -0.1875 to 0.1875
- content_weight: bfloat16 [1152, 1152], P('row', 'col'), may hold values from -0.1875 to 0.1875
- content_offset: float32 [1152], P('col'), may hold values from -3 to 3
- merge_weight: bfloat16 [1152, 1152], P('col', 'row'), may hold values from -1 to 1
- merge_offset: float32 [1152], P('row'), may hold values from -3 to 3
- expand_weight: bfloat16 [1152, 4608], P('row', 'col'), may hold values from -0.1875 to 0.1875
- expand_offset: float32 [4608], P('col'), may hold values from -3 to 3
- shrink_weight: bfloat16 [4608, 1152], P('col', 'row'), may hold values from -0.09375 to 0.09375
- shrink_offset: float32 [1152], P('row'), may hold values from -3 to 3
- cotangent: bfloat16 [2048, 1152], P('col', 'row'), may hold values from -6 to 6
Outputs:
- result: bfloat16 [2048, 1152], P('col', 'row')
- hidden_grad: float32 [2048, 1152], P('col', 'row')
- caption_grad: float32 [1920, 1152], P('col', 'row')
- table_grad: float32 [6, 1152, 1000], P(None, 'row')
- shift_grad: float32 [6, 1152], P(None, 'row')
- query_grad: float32 [1152, 1152], P('row', 'col')
- key_grad: float32 [1152, 1152], P('row', 'col')
- value_grad: float32 [1152, 1152], P('row', 'col')
- output_grad: float32 [1152, 1152], P('col', 'row')
- probe_grad: float32 [1152, 1152], P('row', 'col')
- lookup_grad: float32 [1152, 1152], P('row', 'col')
- content_grad: float32 [1152, 1152], P('row', 'col')
- merge_grad: float32 [1152, 1152], P('col', 'row')
- expand_grad: float32 [1152, 4608], P('row', 'col')
- shrink_grad: float32 [4608, 1152], P('col', 'row')
- offset_query: float32 [1152], P('col')
- offset_value: float32 [1152], P('col')
- offset_output: float32 [1152], P('row')
- offset_probe: float32 [1152], P('col')
- offset_content: float32 [1152], P('col')
- offset_merge: float32 [1152], P('row')
- offset_expand: float32 [4608], P('col')
- offset_shrink: float32 [1152], P('row')
The draws below stay inside these ranges and needn't reach their ends.
Inputs may be any that keep to these rules, and one draw needn't show every extreme that they name: `lengths`: the first latent has all 120 caption tokens and the second one has one.
All inputs are finite; a program needn't handle non-finite values.
Results may differ from the reference program's by a relative error of at most 0.023.
Values may be sent and summed in bfloat16 or wider, within the bound.
No kernel may reach another device: no remote copies, remote signals or barrier semaphores. Data moves between devices by JAX's collectives and lax.ppermute only.
A program may use at most 128 MiB of HBM per device.

```python
import jax
import jax.numpy as jnp
from jax import lax

D = 1152
HDIM = 72
FF = 4608
LTXT = 120
LEN = 128
TSTEPS = 1000
LATENTS = 16
TOKENS = 2048
TEXTS = 1920


def draw_lengths(key, part):
    drawn_lengths = jax.random.randint(key, (LATENTS,), 1, LTXT + 1, dtype=jnp.int32)
    return drawn_lengths.at[0].set(LTXT).at[1].set(1)


def set_ends(entries, stream_key, smallest, high):
    extent = entries.shape
    place = [jax.random.randint(jax.random.fold_in(stream_key, axis), (), 0, extent[axis]) for axis in range(len(extent))]
    entries = entries.at[tuple(place)].set(smallest)
    longest = extent.index(max(extent))
    place[longest] = (place[longest] + 1) % extent[longest]
    return entries.at[tuple(place)].set(high)


def block_levels(own_key, extent, cuts, low, high):
    level = 1.0
    for position, shards_of in cuts:
        draws = jax.random.uniform(jax.random.fold_in(jax.random.fold_in(own_key, 6), position), (shards_of,), jnp.float32, low / len(cuts), high / len(cuts))
        level = level * jnp.repeat(jnp.exp(draws), extent[position] // shards_of).reshape((-1,) + (1,) * (len(extent) - 1 - position))
    return level


def gaussian(rng, extent, width, bound, cuts=(), kind=jnp.bfloat16):
    gain = block_levels(rng, extent, cuts, -0.22, 0.18) if cuts else 1.0
    drawn = jax.random.normal(rng, extent, jnp.float32) * width * gain
    return jnp.minimum(jnp.maximum(drawn, -bound), bound).astype(kind)


def setup_inputs(seed: int = 0) -> dict:
    streams_of = jax.random.split(jax.random.key(seed), 26)
    return {
        "hidden": gaussian(streams_of[0], (TOKENS, D), 1.0, 6.0, ((0, 2), (1, 16))),
        "caption": gaussian(streams_of[1], (TEXTS, D), 1.0, 6.0, ((0, 2), (1, 16))),
        "lengths": draw_lengths(jax.random.fold_in(streams_of[25], 71), 0),
        "timesteps": set_ends(jax.random.randint(streams_of[3], (LATENTS,), 0, TSTEPS), jax.random.fold_in(streams_of[3], 1), 0, TSTEPS - 1).astype(jnp.int32),
        "time_table": gaussian(streams_of[4], (6, D, TSTEPS), 0.3, 2.0, ((1, 16),), jnp.float32),
        "shift_table": gaussian(streams_of[5], (6, D), 0.3, 2.0, ((1, 16),), jnp.float32),
        "query_weight": gaussian(streams_of[6], (D, D), D ** -0.5, 0.1875, ((0, 16), (1, 2))),
        "query_offset": gaussian(streams_of[7], (D,), 0.5, 3.0, ((0, 2),), jnp.float32),
        "key_weight": gaussian(streams_of[8], (D, D), D ** -0.5, 0.1875, ((0, 16), (1, 2))),
        "value_weight": gaussian(streams_of[9], (D, D), D ** -0.5, 0.1875, ((0, 16), (1, 2))),
        "value_offset": gaussian(streams_of[10], (D,), 0.5, 3.0, ((0, 2),), jnp.float32),
        "output_weight": gaussian(streams_of[11], (D, D), (D * 4 // LEN) ** -0.5, 1.0, ((0, 2), (1, 16))),
        "output_offset": gaussian(streams_of[12], (D,), 0.5, 3.0, ((0, 16),), jnp.float32),
        "probe_weight": gaussian(streams_of[13], (D, D), D ** -0.5, 0.1875, ((0, 16), (1, 2))),
        "probe_offset": gaussian(streams_of[14], (D,), 0.5, 3.0, ((0, 2),), jnp.float32),
        "lookup_weight": gaussian(streams_of[15], (D, D), D ** -0.5, 0.1875, ((0, 16), (1, 2))),
        "content_weight": gaussian(streams_of[16], (D, D), D ** -0.5, 0.1875, ((0, 16), (1, 2))),
        "content_offset": gaussian(streams_of[17], (D,), 0.5, 3.0, ((0, 2),), jnp.float32),
        "merge_weight": gaussian(streams_of[18], (D, D), (D * 4 // LTXT) ** -0.5, 1.0, ((0, 2), (1, 16))),
        "merge_offset": gaussian(streams_of[19], (D,), 0.5, 3.0, ((0, 16),), jnp.float32),
        "expand_weight": gaussian(streams_of[20], (D, FF), D ** -0.5, 0.1875, ((0, 16), (1, 2))),
        "expand_offset": gaussian(streams_of[21], (FF,), 0.5, 3.0, ((0, 2),), jnp.float32),
        "shrink_weight": gaussian(streams_of[22], (FF, D), FF ** -0.5, 0.09375, ((0, 2), (1, 16))),
        "shrink_offset": gaussian(streams_of[23], (D,), 0.5, 3.0, ((0, 16),), jnp.float32),
        "cotangent": gaussian(streams_of[24], (TOKENS, D), 1.0, 6.0, ((0, 2), (1, 16))),
    }


EPSILON = 1e-06

def multiply(left_side, right_side):
    return jnp.dot(left_side, right_side, preferred_element_type=jnp.float32)

def multiply_back(left_side, right_side):
    return lax.dot_general(left_side, right_side, (((1,), (1,)), ((), ())), preferred_element_type=jnp.float32)

def multiply_outer(left_side, right_side):
    return lax.dot_general(left_side, right_side, (((0,), (0,)), ((), ())), preferred_element_type=jnp.float32)

def multiply_outer_high(left_side, right_side):
    return lax.dot_general(left_side, right_side, (((0,), (0,)), ((), ())), precision=lax.Precision.HIGHEST)

def rounded(values):
    return lax.optimization_barrier(values.astype(jnp.bfloat16)).astype(jnp.float32)

def activate(values):
    return jax.nn.gelu(values, approximate=True)

def activate_back(values, upstream):
    return jax.vjp(activate, values)[1](upstream)[0]

def normalize(values):
    center = lax.optimization_barrier(jnp.mean(values, axis=1, keepdims=True))
    squares = lax.optimization_barrier(jnp.mean(values * values, axis=1, keepdims=True))
    factor = lax.rsqrt(squares - center * center + EPSILON)
    return ((values - center) * factor, factor)

def normalize_back(upstream, normed, factor):
    first_mean = lax.optimization_barrier(jnp.mean(upstream, axis=1, keepdims=True))
    second_mean = lax.optimization_barrier(jnp.mean(upstream * normed, axis=1, keepdims=True))
    return factor * (upstream - first_mean - normed * second_mean)

def score_block(query_rows, key_rows, valid_keys):
    scores = jnp.einsum('bqhe,bkhe->bhqk', query_rows.astype(jnp.float32), key_rows.astype(jnp.float32)) * HDIM ** (-0.5)
    return jnp.where(valid_keys, scores, -1e+30)

def attend(query_rows, key_rows, value_rows, valid_keys):
    scores = score_block(query_rows, key_rows, valid_keys)
    highest = lax.optimization_barrier(jnp.max(scores, axis=-1, keepdims=True))
    logsum = highest + jnp.log(lax.optimization_barrier(jnp.sum(jnp.exp(scores - highest), axis=-1, keepdims=True)))
    soft_weights = jnp.exp(scores - logsum)
    mixed_rows = jnp.einsum('bhqk,bkhe->bqhe', rounded(soft_weights), value_rows.astype(jnp.float32))
    return (mixed_rows.astype(jnp.bfloat16), logsum)

def attend_back(query_rows, key_rows, value_rows, valid_keys, logsum, upstream):
    soft_weights = jnp.exp(score_block(query_rows, key_rows, valid_keys) - logsum)
    upper = upstream.astype(jnp.float32)
    value_grads = jnp.einsum('bhqk,bqhe->bkhe', rounded(soft_weights), upper)
    weight_grads = jnp.einsum('bqhe,bkhe->bhqk', upper, value_rows.astype(jnp.float32))
    inner_sum = lax.optimization_barrier(jnp.sum(soft_weights * weight_grads, axis=-1, keepdims=True))
    score_grads = rounded(soft_weights * (weight_grads - inner_sum) * HDIM ** (-0.5))
    query_grads = jnp.einsum('bhqk,bkhe->bqhe', score_grads, key_rows.astype(jnp.float32))
    key_grads = jnp.einsum('bhqk,bqhe->bkhe', score_grads, query_rows.astype(jnp.float32))
    return (query_grads, key_grads, value_grads)

def by_latent(values):
    return values.reshape(-1, LEN, values.shape[-1])

def flatten(values):
    return values.reshape(-1, values.shape[-1])

def by_head(values, length):
    return values.reshape(-1, length, values.shape[-1] // HDIM, HDIM)

def modulated(modulation, index):
    return modulation[:, index][:, None, :]

def token_sums(values):
    return lax.optimization_barrier(jnp.sum(by_latent(values), axis=1))

def reference(hidden, caption, lengths, timesteps, time_table, shift_table, query_weight, query_offset, key_weight, value_weight, value_offset, output_weight, output_offset, probe_weight, probe_offset, lookup_weight, content_weight, content_offset, merge_weight, merge_offset, expand_weight, expand_offset, shrink_weight, shrink_offset, cotangent):
    step_picks = (timesteps[:, None] == jnp.arange(TSTEPS, dtype=jnp.int32)[None, :]).astype(jnp.float32)
    modulation = lax.dot_general(step_picks, time_table.reshape(6 * D, TSTEPS), (((1,), (1,)), ((), ())), precision=lax.Precision.HIGHEST).reshape(LATENTS, 6, D) + shift_table[None]
    start = hidden.astype(jnp.float32)
    normed_one, factor_one = normalize(start)
    attend_input = flatten(by_latent(normed_one) * (1.0 + modulated(modulation, 1)) + modulated(modulation, 0)).astype(jnp.bfloat16)
    query_rows = (multiply(attend_input, query_weight) + query_offset).astype(jnp.bfloat16)
    key_rows = multiply(attend_input, key_weight).astype(jnp.bfloat16)
    value_rows = (multiply(attend_input, value_weight) + value_offset).astype(jnp.bfloat16)
    every_key = jnp.ones((1, 1, 1, 1), dtype=jnp.bool_)
    self_mixed, self_logsum = attend(by_head(query_rows, LEN), by_head(key_rows, LEN), by_head(value_rows, LEN), every_key)
    self_mixed = self_mixed.reshape(TOKENS, D)
    branch_self = multiply(self_mixed, output_weight) + output_offset
    after_self = start + flatten(modulated(modulation, 2) * by_latent(branch_self))
    cross_input = after_self.astype(jnp.bfloat16)
    probe_rows = (multiply(cross_input, probe_weight) + probe_offset).astype(jnp.bfloat16)
    lookup_rows = multiply(caption, lookup_weight).astype(jnp.bfloat16)
    content_rows = (multiply(caption, content_weight) + content_offset).astype(jnp.bfloat16)
    valid_text = (jnp.arange(LTXT, dtype=jnp.int32)[None, :] < lengths[:, None])[:, None, None, :]
    cross_mixed, cross_logsum = attend(by_head(probe_rows, LEN), by_head(lookup_rows, LTXT), by_head(content_rows, LTXT), valid_text)
    cross_mixed = cross_mixed.reshape(TOKENS, D)
    branch_cross = multiply(cross_mixed, merge_weight) + merge_offset
    after_cross = after_self + branch_cross
    normed_two, factor_two = normalize(after_cross)
    feed_input = flatten(by_latent(normed_two) * (1.0 + modulated(modulation, 4)) + modulated(modulation, 3)).astype(jnp.bfloat16)
    expanded = multiply(feed_input, expand_weight) + expand_offset
    activated = activate(expanded).astype(jnp.bfloat16)
    branch_feed = multiply(activated, shrink_weight) + shrink_offset
    result = (after_cross + flatten(modulated(modulation, 5) * by_latent(branch_feed))).astype(jnp.bfloat16)
    upstream = cotangent.astype(jnp.float32)
    gate_feed_grad = token_sums(upstream * branch_feed)
    feed_branch_grad = flatten(modulated(modulation, 5) * by_latent(upstream))
    feed_branch_low = feed_branch_grad.astype(jnp.bfloat16)
    shrink_grad = multiply_outer(activated, feed_branch_low)
    offset_shrink = lax.optimization_barrier(jnp.sum(feed_branch_grad, axis=0))
    expanded_grad = activate_back(expanded, multiply_back(feed_branch_low, shrink_weight))
    offset_expand = lax.optimization_barrier(jnp.sum(expanded_grad, axis=0))
    expanded_low = expanded_grad.astype(jnp.bfloat16)
    expand_grad = multiply_outer(feed_input, expanded_low)
    feed_input_grad = multiply_back(expanded_low, expand_weight)
    scale_feed_grad = token_sums(feed_input_grad * normed_two)
    shift_feed_grad = token_sums(feed_input_grad)
    cross_grad = upstream + normalize_back(flatten(by_latent(feed_input_grad) * (1.0 + modulated(modulation, 4))), normed_two, factor_two)
    cross_low = cross_grad.astype(jnp.bfloat16)
    merge_grad = multiply_outer(cross_mixed, cross_low)
    offset_merge = lax.optimization_barrier(jnp.sum(cross_grad, axis=0))
    cross_mixed_grad = multiply_back(cross_low, merge_weight).astype(jnp.bfloat16)
    probe_grads, lookup_grads, content_grads = attend_back(by_head(probe_rows, LEN), by_head(lookup_rows, LTXT), by_head(content_rows, LTXT), valid_text, cross_logsum, by_head(cross_mixed_grad, LEN))
    probe_grads = probe_grads.reshape(TOKENS, D)
    lookup_grads = lookup_grads.reshape(TEXTS, D)
    content_grads = content_grads.reshape(TEXTS, D)
    probe_low = probe_grads.astype(jnp.bfloat16)
    lookup_low = lookup_grads.astype(jnp.bfloat16)
    content_low = content_grads.astype(jnp.bfloat16)
    probe_grad = multiply_outer(cross_input, probe_low)
    lookup_grad = multiply_outer(caption, lookup_low)
    content_grad = multiply_outer(caption, content_low)
    offset_probe = lax.optimization_barrier(jnp.sum(probe_grads, axis=0))
    offset_content = lax.optimization_barrier(jnp.sum(content_grads, axis=0))
    caption_grad = multiply_back(lookup_low, lookup_weight) + multiply_back(content_low, content_weight)
    self_grad = cross_grad + multiply_back(probe_low, probe_weight)
    gate_self_grad = token_sums(self_grad * branch_self)
    self_branch_grad = flatten(modulated(modulation, 2) * by_latent(self_grad))
    self_low = self_branch_grad.astype(jnp.bfloat16)
    output_grad = multiply_outer(self_mixed, self_low)
    offset_output = lax.optimization_barrier(jnp.sum(self_branch_grad, axis=0))
    self_mixed_grad = multiply_back(self_low, output_weight).astype(jnp.bfloat16)
    query_grads, key_grads, value_grads = attend_back(by_head(query_rows, LEN), by_head(key_rows, LEN), by_head(value_rows, LEN), every_key, self_logsum, by_head(self_mixed_grad, LEN))
    query_grads = query_grads.reshape(TOKENS, D)
    key_grads = key_grads.reshape(TOKENS, D)
    value_grads = value_grads.reshape(TOKENS, D)
    query_low = query_grads.astype(jnp.bfloat16)
    key_low = key_grads.astype(jnp.bfloat16)
    value_low = value_grads.astype(jnp.bfloat16)
    query_grad = multiply_outer(attend_input, query_low)
    key_grad = multiply_outer(attend_input, key_low)
    value_grad = multiply_outer(attend_input, value_low)
    offset_query = lax.optimization_barrier(jnp.sum(query_grads, axis=0))
    offset_value = lax.optimization_barrier(jnp.sum(value_grads, axis=0))
    attend_input_grad = multiply_back(query_low, query_weight) + multiply_back(key_low, key_weight) + multiply_back(value_low, value_weight)
    scale_self_grad = token_sums(attend_input_grad * normed_one)
    shift_self_grad = token_sums(attend_input_grad)
    hidden_grad = self_grad + normalize_back(flatten(by_latent(attend_input_grad) * (1.0 + modulated(modulation, 1))), normed_one, factor_one)
    modulation_grad = jnp.stack([shift_self_grad, scale_self_grad, gate_self_grad, shift_feed_grad, scale_feed_grad, gate_feed_grad], axis=1)
    shift_grad = lax.optimization_barrier(jnp.sum(modulation_grad, axis=0))
    table_grad = multiply_outer_high(modulation_grad.reshape(LATENTS, 6 * D), step_picks).reshape(6, D, TSTEPS)
    return (result, hidden_grad, caption_grad, table_grad, shift_grad, query_grad, key_grad, value_grad, output_grad, probe_grad, lookup_grad, content_grad, merge_grad, expand_grad, shrink_grad, offset_query, offset_value, offset_output, offset_probe, offset_content, offset_merge, offset_expand, offset_shrink)
```

```python
import jax
import jax.numpy as jnp
from jax import lax
from jax.sharding import PartitionSpec as P

D = 1152
HDIM = 72
LTXT = 120
LEN = 128
TSTEPS = 1000


EPSILON = 1e-06


def multiply(left_side, right_side):
    return jnp.dot(left_side, right_side, preferred_element_type=jnp.float32)


def multiply_back(left_side, right_side):
    return lax.dot_general(
        left_side, right_side, (((1,), (1,)), ((), ())), preferred_element_type=jnp.float32
    )


def multiply_outer(left_side, right_side):
    return lax.dot_general(
        left_side, right_side, (((0,), (0,)), ((), ())), preferred_element_type=jnp.float32
    )


def activate(values):
    return jax.nn.gelu(values, approximate=True)


def activate_back(values, upstream):
    return jax.vjp(activate, values)[1](upstream)[0]


def score_block(query_rows, key_rows, valid_keys):
    scores = jnp.einsum(
        "bqhe,bkhe->bhqk", query_rows, key_rows, preferred_element_type=jnp.float32
    ) * HDIM ** (-0.5)
    return jnp.where(valid_keys, scores, -1e30)


def attend(query_rows, key_rows, value_rows, valid_keys):
    scores = score_block(query_rows, key_rows, valid_keys)
    highest = jnp.max(scores, axis=-1, keepdims=True)
    logsum = highest + jnp.log(jnp.sum(jnp.exp(scores - highest), axis=-1, keepdims=True))
    soft_weights = jnp.exp(scores - logsum).astype(jnp.bfloat16)
    mixed_rows = jnp.einsum(
        "bhqk,bkhe->bqhe", soft_weights, value_rows, preferred_element_type=jnp.float32
    )
    return (mixed_rows.astype(jnp.bfloat16), logsum)


def attend_back(query_rows, key_rows, value_rows, valid_keys, logsum, upstream):
    soft_weights = jnp.exp(score_block(query_rows, key_rows, valid_keys) - logsum)
    value_grads = jnp.einsum(
        "bhqk,bqhe->bkhe",
        soft_weights.astype(jnp.bfloat16),
        upstream,
        preferred_element_type=jnp.float32,
    )
    weight_grads = jnp.einsum(
        "bqhe,bkhe->bhqk", upstream, value_rows, preferred_element_type=jnp.float32
    )
    inner_sum = jnp.sum(soft_weights * weight_grads, axis=-1, keepdims=True)
    score_grads = (soft_weights * (weight_grads - inner_sum) * HDIM ** (-0.5)).astype(jnp.bfloat16)
    query_grads = jnp.einsum(
        "bhqk,bkhe->bqhe", score_grads, key_rows, preferred_element_type=jnp.float32
    )
    key_grads = jnp.einsum(
        "bhqk,bqhe->bkhe", score_grads, query_rows, preferred_element_type=jnp.float32
    )
    return (query_grads, key_grads, value_grads)


LANES = 128


def padded(values):
    return jnp.pad(values, ((0, 0), (0, -values.shape[1] % LANES)))


def pack(pieces):
    starts = []
    width = 0
    blocks = []
    for piece in pieces:
        blocks.append(padded(piece))
        starts.append((width, width + piece.shape[1]))
        width += blocks[-1].shape[1]
    return (jnp.concatenate(blocks, axis=1), starts)


def unpack(packed, starts):
    return [packed[:, low:high] for low, high in starts]


def gather_rows(values):
    return lax.all_gather(values, "row", axis=0, tiled=True)


def col_sum(partial):
    if lax.axis_size("col") == 2:
        other = lax.ppermute(partial.astype(jnp.bfloat16), "col", [(0, 1), (1, 0)])
        return partial + other.astype(jnp.float32)
    return lax.psum(partial, "col")


def two_parts(values):
    high = values.astype(jnp.bfloat16)
    low = (values - high.astype(jnp.float32)).astype(jnp.bfloat16)
    return (high, low)


def feature_mean(values):
    return jnp.sum(values, axis=-1, keepdims=True) / D


def normalize(values):
    center = feature_mean(values)
    factor = lax.rsqrt(feature_mean(values * values) - center * center + EPSILON)
    return ((values - center) * factor, factor)


def normalize_back(upstream, normed, factor):
    return factor * (upstream - feature_mean(upstream) - normed * feature_mean(upstream * normed))


def by_head(values, length):
    return values.reshape(-1, length, values.shape[-1] // HDIM, HDIM)


def flat(values):
    return values.reshape(-1, values.shape[-1])


def to_token_rows(values):
    size = lax.axis_size("row")
    moved = lax.all_to_all(values, "row", 0, 0, tiled=True)
    moved = moved.reshape(size, -1, *moved.shape[1:]).transpose(1, 2, 0, 3)
    return moved.reshape(*moved.shape[:2], -1)


def to_features(values):
    size = lax.axis_size("row")
    own, rows, width = values.shape
    parts = values.reshape(own, rows, size, width // size).transpose(2, 0, 1, 3)
    return lax.all_to_all(parts.reshape(size * own, rows, -1), "row", 0, 0, tiled=True)


def outer_with_sum(sources, upstream):
    width = sources.shape[1]
    ones = jnp.ones((sources.shape[0], 1), jnp.bfloat16)
    wide = jnp.concatenate([sources, ones], axis=1)
    product = multiply_outer(jnp.pad(wide, ((0, 0), (0, -wide.shape[1] % 8))), upstream)
    return (product[:width], product[width])


def per_device(
    hidden,
    caption,
    lengths,
    timesteps,
    time_table,
    shift_table,
    query_weight,
    query_offset,
    key_weight,
    value_weight,
    value_offset,
    output_weight,
    output_offset,
    probe_weight,
    probe_offset,
    lookup_weight,
    content_weight,
    content_offset,
    merge_weight,
    merge_offset,
    expand_weight,
    expand_offset,
    shrink_weight,
    shrink_offset,
    cotangent,
):
    low = jnp.bfloat16
    width = hidden.shape[1]
    heads_width = query_weight.shape[1]
    latents = timesteps.shape[0]
    own = latents // lax.axis_size("row")
    col_latents = hidden.shape[0] // LEN

    near_pack, near_starts = pack(
        [
            jnp.concatenate([query_weight, key_weight, value_weight], axis=1),
            output_weight.T,
            probe_weight,
            jnp.concatenate([lookup_weight, content_weight], axis=1),
            merge_weight.T,
        ]
    )
    far_pack, far_starts = pack([expand_weight, shrink_weight.T])
    near_full = gather_rows(near_pack)

    picks = (timesteps[:, None] == jnp.arange(TSTEPS, dtype=jnp.int32)[None, :]).astype(
        jnp.float32
    )
    own_modulation = (
        lax.dot_general(
            picks,
            time_table.reshape(6 * width, TSTEPS),
            (((1,), (1,)), ((), ())),
            precision=lax.Precision.HIGHEST,
        ).reshape(latents, 6, width)
        + shift_table[None]
    )
    whole = lax.all_gather(
        jnp.concatenate([hidden, cotangent, caption], axis=0), "col", axis=0, tiled=False
    )
    tokens = hidden.shape[0]
    hidden_all = whole[:, :tokens].reshape(latents, LEN, width)
    cotangent_all = whole[:, tokens : 2 * tokens].reshape(latents, LEN, width)
    caption_all = whole[:, 2 * tokens :].reshape(latents, LTXT, width)
    offsets = jnp.stack([output_offset, merge_offset, shrink_offset])[None]
    small = jnp.concatenate([own_modulation, jnp.broadcast_to(offsets, (latents, 3, width))], axis=1)
    arrived = to_token_rows(
        jnp.concatenate([hidden_all, cotangent_all, caption_all, *two_parts(small)], axis=1)
    )
    far_pack, arrived = lax.optimization_barrier((far_pack, arrived))
    far_full = gather_rows(far_pack)

    start = flat(arrived[:, :LEN]).astype(jnp.float32)
    upstream = flat(arrived[:, LEN : 2 * LEN]).astype(jnp.float32)
    text = flat(arrived[:, 2 * LEN : 2 * LEN + LTXT])
    tail = arrived[:, 2 * LEN + LTXT :].astype(jnp.float32)
    modulation = tail[:, :9] + tail[:, 9:]
    output_bias, merge_bias, shrink_bias = (modulation[0, 6 + i][None] for i in range(3))

    def spread(index):
        rows = jnp.broadcast_to(modulation[:, index][:, None], (own, LEN, D))
        return flat(rows)

    def latent_sums(values):
        return jnp.sum(values.reshape(own, LEN, -1), axis=1)

    shift_a, scale_a, gate_a, shift_f, scale_f, gate_f = (spread(i) for i in range(6))
    qkv_weight, output_flip, probe_full, text_weight, merge_flip = unpack(near_full, near_starts)
    expand_full, shrink_flip = unpack(far_full, far_starts)

    normed_one, factor_one = normalize(start)
    attend_input = (normed_one * (1.0 + scale_a) + shift_a).astype(low)
    no_offset = jnp.zeros_like(query_offset)
    qkv_rows = (
        multiply(attend_input, qkv_weight)
        + jnp.concatenate([query_offset, no_offset, value_offset])[None]
    ).astype(low)
    query_rows, key_rows, value_rows = (
        by_head(qkv_rows[:, i * heads_width : (i + 1) * heads_width], LEN) for i in range(3)
    )
    text_rows = (
        multiply(text, text_weight) + jnp.concatenate([no_offset, content_offset])[None]
    ).astype(low)
    lookup_rows = by_head(text_rows[:, :heads_width], LTXT)
    content_rows = by_head(text_rows[:, heads_width:], LTXT)
    own_lengths = lax.dynamic_slice_in_dim(lengths, lax.axis_index("row") * own, own)
    valid_text = (jnp.arange(LTXT, dtype=jnp.int32)[None, :] < own_lengths[:, None])[
        :, None, None, :
    ]
    every_key = jnp.ones((1, 1, 1, 1), dtype=jnp.bool_)
    self_mixed, self_logsum = attend(query_rows, key_rows, value_rows, every_key)
    self_mixed = self_mixed.reshape(-1, heads_width)
    branch_self = col_sum(multiply_back(self_mixed, output_flip)) + output_bias
    after_self = start + gate_a * branch_self
    cross_input = after_self.astype(low)
    probe_rows = by_head((multiply(cross_input, probe_full) + probe_offset).astype(low), LEN)
    cross_mixed, cross_logsum = attend(probe_rows, lookup_rows, content_rows, valid_text)
    cross_mixed = cross_mixed.reshape(-1, heads_width)
    branch_cross = col_sum(multiply_back(cross_mixed, merge_flip)) + merge_bias
    after_cross = after_self + branch_cross
    normed_two, factor_two = normalize(after_cross)
    feed_input = (normed_two * (1.0 + scale_f) + shift_f).astype(low)
    expanded = multiply(feed_input, expand_full) + expand_offset
    activated = activate(expanded).astype(low)
    first_pack, first_starts = pack([activated, self_mixed, cross_mixed])
    first_full = gather_rows(first_pack)

    feed_branch_grad = gate_f * upstream
    activated_grad = multiply(feed_branch_grad.astype(low), shrink_flip)
    expanded_grad = activate_back(expanded, activated_grad).astype(low)
    feed_input_grad = col_sum(multiply_back(expanded_grad, expand_full))
    cross_grad = upstream + normalize_back(
        feed_input_grad * (1.0 + scale_f), normed_two, factor_two
    )
    cross_low = cross_grad.astype(low)
    cross_mixed_grad = multiply(cross_low, merge_flip).astype(low)
    probe_grads, lookup_grads, content_grads = attend_back(
        probe_rows,
        lookup_rows,
        content_rows,
        valid_text,
        cross_logsum,
        by_head(cross_mixed_grad, LEN),
    )
    probe_grads = probe_grads.reshape(-1, heads_width).astype(low)
    text_grads = jnp.concatenate(
        [lookup_grads.reshape(-1, heads_width), content_grads.reshape(-1, heads_width)], axis=1
    ).astype(low)
    self_grad = cross_grad + col_sum(multiply_back(probe_grads, probe_full))
    self_branch_grad = gate_a * self_grad
    self_branch_low = self_branch_grad.astype(low)
    self_mixed_grad = multiply(self_branch_low, output_flip).astype(low)
    qkv_grads = attend_back(
        query_rows, key_rows, value_rows, every_key, self_logsum, by_head(self_mixed_grad, LEN)
    )
    qkv_grads = jnp.concatenate(
        [part.reshape(-1, heads_width).astype(low) for part in qkv_grads], axis=1
    )
    text_wide = jnp.pad(text_grads.reshape(own, LTXT, -1), ((0, 0), (0, LEN - LTXT), (0, 0)))
    second_pack, second_starts = pack([expanded_grad, qkv_grads, probe_grads, flat(text_wide)])
    second_full = gather_rows(second_pack)

    branch_feed = col_sum(multiply_back(activated, shrink_flip)) + shrink_bias
    result = after_cross + gate_f * branch_feed
    caption_grad = col_sum(multiply_back(text_grads, text_weight))
    attend_input_grad = col_sum(multiply_back(qkv_grads, qkv_weight))
    hidden_grad = self_grad + normalize_back(
        attend_input_grad * (1.0 + scale_a), normed_one, factor_one
    )
    modulation_grad = jnp.stack(
        [
            latent_sums(attend_input_grad),
            latent_sums(attend_input_grad * normed_one),
            latent_sums(self_grad * branch_self),
            latent_sums(feed_input_grad),
            latent_sums(feed_input_grad * normed_two),
            latent_sums(upstream * branch_feed),
        ],
        axis=1,
    )

    def rows_of(values, length):
        return values.astype(low).reshape(own, length, D)

    returned = to_features(
        jnp.concatenate(
            [
                rows_of(result, LEN),
                rows_of(hidden_grad, LEN),
                rows_of(attend_input, LEN),
                rows_of(cross_input, LEN),
                rows_of(feed_input, LEN),
                rows_of(cross_grad, LEN),
                rows_of(self_branch_grad, LEN),
                rows_of(caption_grad, LTXT),
                *two_parts(modulation_grad),
            ],
            axis=1,
        )
    )
    col_first = lax.axis_index("col") * col_latents
    here = lax.dynamic_slice_in_dim(returned, col_first, col_latents)
    features = [flat(returned[:, i * LEN : (i + 1) * LEN]) for i in range(7)]
    base = 7 * LEN
    sums = returned[:, base + LTXT :].astype(jnp.float32)
    every_modulation = sums[:, :6] + sums[:, 6:]
    table_grad = lax.dot_general(
        every_modulation.reshape(latents, 6 * width),
        picks,
        (((0,), (0,)), ((), ())),
        precision=lax.Precision.HIGHEST,
    ).reshape(6, width, TSTEPS)
    own_branch_grad = own_modulation[:, 5][:, None] * cotangent_all.astype(jnp.float32)

    activated_full, self_mixed_full, cross_mixed_full = unpack(first_full, first_starts)
    expanded_full, qkv_full, probe_grads_full, text_full = unpack(second_full, second_starts)
    shrink_grad = multiply_outer(activated_full, flat(own_branch_grad).astype(low))
    output_grad = multiply_outer(self_mixed_full, features[6])
    merge_grad = multiply_outer(cross_mixed_full, features[5])
    expand_grad, offset_expand = outer_with_sum(features[4], expanded_full)
    qkv_grad, offset_qkv = outer_with_sum(features[2], qkv_full)
    probe_grad, offset_probe = outer_with_sum(features[3], probe_grads_full)
    caption_wide = jnp.pad(caption_all, ((0, 0), (0, LEN - LTXT), (0, 0)))
    text_grad, offset_text = outer_with_sum(flat(caption_wide), text_full)

    def third(values, index):
        return values[..., index * heads_width : (index + 1) * heads_width]

    def token_sum(values):
        return jnp.sum(values.astype(jnp.float32), axis=0)

    return (
        flat(here[:, :LEN]),
        flat(here[:, LEN : 2 * LEN]).astype(jnp.float32),
        flat(here[:, base : base + LTXT]).astype(jnp.float32),
        table_grad,
        jnp.sum(every_modulation, axis=0),
        third(qkv_grad, 0),
        third(qkv_grad, 1),
        third(qkv_grad, 2),
        output_grad,
        probe_grad,
        third(text_grad, 0),
        third(text_grad, 1),
        merge_grad,
        expand_grad,
        shrink_grad,
        third(offset_qkv, 0),
        third(offset_qkv, 2),
        token_sum(features[6]),
        offset_probe,
        third(offset_text, 1),
        token_sum(features[5]),
        offset_expand,
        jnp.sum(flat(own_branch_grad), axis=0),
    )


def solution(mesh):
    return jax.shard_map(
        per_device,
        mesh=mesh,
        in_specs=(
            P("col", "row"),
            P("col", "row"),
            P(),
            P(),
            P(None, "row", None),
            P(None, "row"),
            P("row", "col"),
            P("col"),
            P("row", "col"),
            P("row", "col"),
            P("col"),
            P("col", "row"),
            P("row"),
            P("row", "col"),
            P("col"),
            P("row", "col"),
            P("row", "col"),
            P("col"),
            P("col", "row"),
            P("row"),
            P("row", "col"),
            P("col"),
            P("col", "row"),
            P("row"),
            P("col", "row"),
        ),
        out_specs=(
            P("col", "row"),
            P("col", "row"),
            P("col", "row"),
            P(None, "row", None),
            P(None, "row"),
            P("row", "col"),
            P("row", "col"),
            P("row", "col"),
            P("col", "row"),
            P("row", "col"),
            P("row", "col"),
            P("row", "col"),
            P("col", "row"),
            P("row", "col"),
            P("col", "row"),
            P("col"),
            P("col"),
            P("row"),
            P("col"),
            P("col"),
            P("row"),
            P("col"),
            P("row"),
        ),
        check_vma=False,
    )
```
